32 devices in a mesh: dp: 8 (over y, x, core), seq: 4 (over z).
Axes of the slice: x: 2, y: 2, z: 4, core: 2. Of those that a mesh axis runs over, the one named last changes fastest.
Arguments:
- tokens: bfloat16 [16, 1024, 1280], P('dp', 'seq'), may hold values from -6 to 6
- lengths: int32 [16], P('dp'), may hold values from 204 to 1024, as said below
- cotangent: bfloat16 [16, 1024, 1280], P('dp', 'seq'), may hold values from -6 to 6
- w_qkv: bfloat16 [1280, 3840], P(('dp', 'seq')), may hold values from -0.15625 to 0.15625
- w_out: bfloat16 [1280, 1280], P(('dp', 'seq')), may hold values from -2.5 to 2.5
- w_up: bfloat16 [1280, 5120], P(('dp', 'seq')), may hold values from -0.15625 to 0.15625
- w_down: bfloat16 [5120, 1280], P(('dp', 'seq')), may hold values from -0.078125 to 0.078125
- gain_one: bfloat16 [1280], P(('dp', 'seq')), may hold values from 0.099609375 to 1.8984375
- shift_one: bfloat16 [1280], P(('dp', 'seq')), may hold values from -3 to 3
- bias_query: bfloat16 [1280], P(('dp', 'seq')), may hold values from -3 to 3
- bias_value: bfloat16 [1280], P(('dp', 'seq')), may hold values from -3 to 3
- bias_out: bfloat16 [1280], P(('dp', 'seq')), may hold values from -3 to 3
- gain_two: bfloat16 [1280], P(('dp', 'seq')), may hold values from 0.099609375 to 1.8984375
- shift_two: bfloat16 [1280], P(('dp', 'seq')), may hold values from -3 to 3
- bias_up: bfloat16 [5120], P(('dp', 'seq')), may hold values from -3 to 3
- bias_down: bfloat16 [1280], P(('dp', 'seq')), may hold values from -3 to 3
Outputs:
- output: bfloat16 [16, 1024, 1280], P('dp', 'seq')
- input_grad: float32 [16, 1024, 1280], P('dp', 'seq')
- grad_qkv: float32 [1280, 3840], P(('dp', 'seq'))
- grad_out: float32 [1280, 1280], P(('dp', 'seq'))
- grad_up: float32 [1280, 5120], P(('dp', 'seq'))
- grad_down: float32 [5120, 1280], P(('dp', 'seq'))
- grad_gain_one: float32 [1280], P(('dp', 'seq'))
- grad_shift_one: float32 [1280], P(('dp', 'seq'))
- grad_bias_query: float32 [1280], P(('dp', 'seq'))
- grad_bias_value: float32 [1280], P(('dp', 'seq'))
- grad_bias_out: float32 [1280], P(('dp', 'seq'))
- grad_gain_two: float32 [1280], P(('dp', 'seq'))
- grad_shift_two: float32 [1280], P(('dp', 'seq'))
- grad_bias_up: float32 [5120], P(('dp', 'seq'))
- grad_bias_down: float32 [1280], P(('dp', 'seq'))
The draws below stay inside these ranges and needn't reach their ends.
Inputs may be any that keep to these rules, and one draw needn't show every extreme that they name: Cell c holds genes at positions 0 to lengths[c]-1; the rest up to 1024 is padding that is masked as keys. Some cell has all 1024 positions.
All inputs are finite; a program needn't handle non-finite values.
Results may differ from the reference program's by a relative error of at most 0.03.
Values may be sent and summed in bfloat16 or wider, within the bound.
No kernel may reach another device: no remote copies, remote signals or barrier semaphores. Data moves between devices by JAX's collectives and lax.ppermute only.
A program may use at most 224 MiB of HBM per device.

```python
import math
import jax
import jax.numpy as jnp
from jax import lax

D = 1280
HEADS = 20
HEAD_DIM = 64
FF = 5120
GENES = 1024
CELLS = 16


def draw_lengths(key, part):
    split_one, split_two = jax.random.split(jax.random.fold_in(key, 17))
    lengths_drawn = jax.random.randint(split_one, (CELLS,), GENES // 5, GENES + 1)
    chosen_cell = jax.random.randint(split_two, (), 0, CELLS)
    return jnp.where(jnp.arange(CELLS) == chosen_cell, GENES, lengths_drawn).astype(jnp.int32)


def level_of(key, extent, cuts, low, top_value):
    factor_of = 1.0
    for position, shards_of in cuts:
        steps = jax.random.uniform(jax.random.fold_in(jax.random.fold_in(key, 6), position), (shards_of,), jnp.float32, low / len(cuts), top_value / len(cuts))
        factor_of = factor_of * jnp.repeat(jnp.exp(steps), extent[position] // shards_of).reshape((-1,) + (1,) * (len(extent) - 1 - position))
    return factor_of


def noise(key, extent, spread, most, shards=(), dtype=jnp.bfloat16):
    values = spread * jax.random.normal(key, extent, jnp.float32)
    if shards:
        values = values * level_of(key, extent, shards, -0.22, 0.18)
    return jnp.clip(values, -most, most).astype(dtype)


def setup_inputs(seed: int = 0) -> dict:
    key_of = jax.random.split(jax.random.key(seed), 17)
    return {
        "tokens": noise(key_of[0], (CELLS, GENES, D), 1.0, 6.0, ((0, 8), (1, 4))),
        "lengths": draw_lengths(jax.random.fold_in(key_of[16], 71), 0),
        "cotangent": noise(key_of[2], (CELLS, GENES, D), 1.0, 6.0, ((0, 8), (1, 4))),
        "w_qkv": noise(key_of[3], (D, 3 * D), D ** -0.5, 0.15625, ((0, 32),)),
        "w_out": noise(key_of[4], (D, D), (D * 4 // GENES) ** -0.5, 2.5, ((0, 32),)),
        "w_up": noise(key_of[5], (D, FF), D ** -0.5, 0.15625, ((0, 32),)),
        "w_down": noise(key_of[6], (FF, D), FF ** -0.5, 0.078125, ((0, 32),)),
        "gain_one": jnp.clip(1.0 + 0.18 * jax.random.normal(key_of[7], (D,), jnp.float32), 0.099609375, 1.8984375).astype(jnp.bfloat16),
        "shift_one": noise(key_of[8], (D,), 0.5, 3.0, ((0, 32),)),
        "bias_query": noise(key_of[9], (D,), 0.5, 3.0, ((0, 32),)),
        "bias_value": noise(key_of[10], (D,), 0.5, 3.0, ((0, 32),)),
        "bias_out": noise(key_of[11], (D,), 0.5, 3.0, ((0, 32),)),
        "gain_two": jnp.clip(1.0 + 0.18 * jax.random.normal(key_of[12], (D,), jnp.float32), 0.099609375, 1.8984375).astype(jnp.bfloat16),
        "shift_two": noise(key_of[13], (D,), 0.5, 3.0, ((0, 32),)),
        "bias_up": noise(key_of[14], (FF,), 0.5, 3.0, ((0, 32),)),
        "bias_down": noise(key_of[15], (D,), 0.5, 3.0, ((0, 32),)),
    }


EPSILON = 1e-05
precise = lax.Precision.HIGHEST

@jax.custom_vjp
def low(v):
    return lax.optimization_barrier(v.astype(jnp.bfloat16)).astype(jnp.float32)

@jax.custom_vjp
def low_back(v):
    return v

def low_keep(v):
    return (low(v), None)

def low_pass(kept, grad):
    return (grad,)

def back_keep(v):
    return (v, None)

def back_low(kept, grad):
    return (low(grad),)
low.defvjp(low_keep, low_pass)
low_back.defvjp(back_keep, back_low)

def layer_norm(values, gain, shift):
    row_mean = lax.optimization_barrier(jnp.mean(values, axis=-1, keepdims=True))
    centered = values - row_mean
    variance = lax.optimization_barrier(jnp.mean(centered * centered, axis=-1, keepdims=True))
    return centered * lax.rsqrt(variance + EPSILON) * gain + shift

def gelu_exact(values):
    return jax.nn.gelu(values, approximate=False)

def matmul(left, right):
    return jnp.matmul(left, right, precision=precise)

def block_forward(weights, inputs, counts):
    w_qkv, w_out, w_up, w_down, gain_one, shift_one, bias_query, bias_value, bias_out, gain_two, shift_two, bias_up, bias_down = weights
    group = inputs.shape[0]
    normed = low(layer_norm(inputs, gain_one, shift_one))
    project = matmul(normed, w_qkv)
    queries = low(low_back(project[..., :D] + bias_query))
    keys_part = low(low_back(project[..., D:2 * D]))
    values = low(low_back(project[..., 2 * D:] + bias_value))
    shape_heads = (group, GENES, HEADS, HEAD_DIM)
    scores = jnp.einsum('gqhe,gkhe->ghqk', queries.reshape(shape_heads), keys_part.reshape(shape_heads), precision=precise) * HEAD_DIM ** (-0.5)
    scores = low_back(scores)
    valid = jnp.arange(GENES)[None, :] < counts[:, None]
    scores = jnp.where(valid[:, None, None, :], scores, -1000000000.0)
    soft = low(jax.nn.softmax(scores, axis=-1))
    mixed = jnp.einsum('ghqk,gkhe->gqhe', soft, values.reshape(shape_heads), precision=precise)
    mixed = low(low_back(mixed.reshape(group, GENES, D)))
    attended = low_back(matmul(mixed, w_out) + bias_out)
    middle = inputs + attended
    normed_two = low(layer_norm(middle, gain_two, shift_two))
    hidden = low_back(matmul(normed_two, w_up) + bias_up)
    active = low(gelu_exact(hidden))
    branch = low_back(matmul(active, w_down) + bias_down)
    return middle + branch

def reference(tokens, lengths, cotangent, w_qkv, w_out, w_up, w_down, gain_one, shift_one, bias_query, bias_value, bias_out, gain_two, shift_two, bias_up, bias_down):
    weights = tuple((member.astype(jnp.float32) for member in (w_qkv, w_out, w_up, w_down, gain_one, shift_one, bias_query, bias_value, bias_out, gain_two, shift_two, bias_up, bias_down)))
    inputs = tokens.astype(jnp.float32)
    incoming = cotangent.astype(jnp.float32)
    group = math.gcd(CELLS, 2)

    def forward(params, values):

        def one_group(carry, pieces):
            return (carry, jax.checkpoint(block_forward)(params, pieces[0], pieces[1]))
        _, result = lax.scan(one_group, None, (values.reshape(CELLS // group, group, GENES, D), lengths.reshape(CELLS // group, group)))
        return result.reshape(CELLS, GENES, D)
    output, pullback = jax.vjp(forward, weights, inputs)
    grads, input_grad = pullback(incoming)
    return (output.astype(jnp.bfloat16), input_grad, grads[0], grads[1], grads[2], grads[3], grads[4], grads[5], grads[6], grads[7], grads[8], grads[9], grads[10], grads[11], grads[12])
```

```python
import jax
import jax.numpy as jnp
from jax import lax
from jax.experimental import pallas as pl
from jax.experimental.pallas import tpu as pltpu
from jax.sharding import Mesh
from jax.sharding import PartitionSpec as P

HEADS = 20
EPSILON = 1e-05
NEG = -1000000000.0
QB = 256
BF = jnp.bfloat16
F32 = jnp.float32
ALL = ("ya", "xb", "core", "seq")
DP = ("ya", "xb", "core")


def dot(left, right, dims, out=F32):
    return lax.dot_general(left, right, (dims, ((), ())), preferred_element_type=out)


NN = ((1,), (0,))
NT = ((1,), (1,))
TN = ((0,), (0,))


def size(name):
    return lax.axis_size(name)


def swap(values):
    return lax.ppermute(values, "core", [(0, 1), (1, 0)])


def by_core(own, other, axis):
    low = jnp.concatenate([own, other], axis=axis)
    high = jnp.concatenate([other, own], axis=axis)
    return jnp.where(lax.axis_index("core") == 0, low, high)


def pick(values, axis, which):
    return lax.dynamic_index_in_dim(values, which, axis, keepdims=False)


def normalise(values):
    mean = jnp.mean(values, axis=-1, keepdims=True)
    centered = values - mean
    inverse = lax.rsqrt(jnp.mean(centered * centered, axis=-1, keepdims=True) + EPSILON)
    return centered * inverse, inverse


def norm_back(normal, inverse, incoming, gain):
    scaled = incoming * gain
    first = jnp.mean(scaled, axis=-1, keepdims=True)
    second = jnp.mean(scaled * normal, axis=-1, keepdims=True)
    return (scaled - first - normal * second) * inverse


def route(cells, chips, step):
    pairs = []
    for core in range(2):
        for place in range(chips):
            block = (place + step) % chips
            target = (block // cells) * chips + core * cells + block % cells
            pairs.append((core * chips + place, target))
    return pairs


def to_cells(values):
    cells, rows, width = values.shape
    chips = size("seq")
    core, place = lax.axis_index("core"), lax.axis_index("seq")
    blocks = values.reshape(cells, 2, rows // 2, width).transpose(1, 0, 2, 3)
    blocks = blocks.reshape(chips, rows // 2, width)
    mine = core * cells + place % cells
    parts = []
    for step in range(chips):
        piece = pick(blocks, 0, (place + step) % chips)
        parts.append(lax.ppermute(piece, ("core", "seq"), route(cells, chips, step)))
    result = jnp.zeros((chips, rows // 2, width), values.dtype)
    for step in range(chips):
        slot = (mine - step + chips) % chips
        result = lax.dynamic_update_slice_in_dim(result, parts[step][None], slot, 0)
    return result.reshape(chips * rows // 2, width)


def from_cells(values, cells):
    chips = size("seq")
    core, place = lax.axis_index("core"), lax.axis_index("seq")
    rows = 2 * values.shape[0] // chips
    width = values.shape[1]
    blocks = values.reshape(chips, rows // 2, width)
    mine = core * cells + place % cells
    result = jnp.zeros((chips, rows // 2, width), values.dtype)
    parts = []
    for step in range(chips):
        piece = pick(blocks, 0, (mine - step + chips) % chips)
        back = [(b, a) for a, b in route(cells, chips, step)]
        parts.append(lax.ppermute(piece, ("core", "seq"), back))
    for step in range(chips):
        slot = (place + step) % chips
        result = lax.dynamic_update_slice_in_dim(result, parts[step][None], slot, 0)
    result = result.reshape(2, cells, rows // 2, width).transpose(1, 0, 2, 3)
    return result.reshape(cells, rows, width)


def reduce_axis(values, axis, name):
    count = size(name)
    if count > 4:
        return lax.psum_scatter(values, name, scatter_dimension=axis, tiled=False)
    index = lax.axis_index(name)
    parts = []
    for step in range(1, count):
        piece = pick(values, axis, (index + step) % count)
        pairs = [(j, (j + step) % count) for j in range(count)]
        parts.append(lax.ppermute(piece, name, pairs))
    total = pick(values, axis, index).astype(F32)
    for part in parts:
        total = total + part.astype(F32)
    return total.astype(values.dtype)


def reduce_chips(values, seq_axis):
    half = values.shape[-1] // 2
    first = reduce_axis(reduce_axis(values[..., :half], 0, "ya"), 0, "xb")
    second = reduce_axis(reduce_axis(values[..., half:], 1, "xb"), 0, "ya")
    first = reduce_axis(first, seq_axis, "seq")
    second = reduce_axis(second, seq_axis, "seq")
    return jnp.concatenate([first, second], axis=-1)


def reduce_columns(grad, parts):
    ya, xb, chips = size("ya"), size("xb"), size("seq")
    rows = grad.shape[0] // (ya * xb * 2 * chips)
    core = lax.axis_index("core")
    done = reduce_chips(grad.reshape(ya, xb, 2, chips, rows, -1), 1)
    own = pick(done, 0, core).reshape(rows, parts, 1, -1)
    other = swap(pick(done, 0, 1 - core)).reshape(rows, parts, 1, -1)
    return by_core(own, other, 2).reshape(rows, -1).astype(F32)


def forward_kernel(q_ref, k_ref, v_ref, mask_ref, o_ref, lse_ref):
    rows, lanes = q_ref.shape
    dim = lanes // 2
    scale = dim ** (-0.5)
    valid = mask_ref[...] > 0
    for head in range(2):
        part = slice(head * dim, (head + 1) * dim)
        keys = k_ref[:, part]
        turned = v_ref[:, part].T

        def block(index, carry):
            start = pl.multiple_of(index * QB, QB)
            queries = q_ref[pl.ds(start, QB), part] * BF(scale)
            scores = jnp.where(valid, dot(keys, queries, NT), NEG)
            top = jnp.max(scores, axis=0, keepdims=True)
            exponent = jnp.exp(scores - top)
            total = jnp.sum(exponent, axis=0, keepdims=True)
            mixed = dot(turned, exponent.astype(BF), NN) / total
            o_ref[pl.ds(start, QB), part] = mixed.T.astype(BF)
            lse_ref[0, head : head + 1, pl.ds(start, QB)] = top + jnp.log(total)
            return carry

        lax.fori_loop(0, rows // QB, block, 0)


def backward_kernel(q_ref, k_ref, v_ref, d_ref, lse_ref, mask_ref, out_ref, dk_ref, dv_ref):
    rows, lanes = q_ref.shape
    dim = lanes // 2
    scale = dim ** (-0.5)
    valid = mask_ref[...] > 0
    for head in range(2):
        part = slice(head * dim, (head + 1) * dim)
        keys = k_ref[:, part]
        values = v_ref[:, part]
        turned = keys.T
        dk_ref[...] = jnp.zeros_like(dk_ref)
        dv_ref[...] = jnp.zeros_like(dv_ref)

        def block(index, carry):
            start = pl.multiple_of(index * QB, QB)
            queries = q_ref[pl.ds(start, QB), part] * BF(scale)
            incoming = d_ref[pl.ds(start, QB), part]
            lse = lse_ref[0, head : head + 1, pl.ds(start, QB)]
            scores = jnp.where(valid, dot(keys, queries, NT), NEG)
            soft = jnp.exp(scores - lse)
            d_soft = dot(values, incoming, NT)
            inner = jnp.sum(soft * d_soft, axis=0, keepdims=True)
            d_scores = (soft * (d_soft - inner)).astype(BF)
            dv_ref[...] += dot(soft.astype(BF), incoming, NN)
            dk_ref[...] += dot(d_scores, queries, NN)
            d_queries = dot(turned, d_scores, NN) * scale
            out_ref[0, pl.ds(start, QB), part] = d_queries.T.astype(BF)
            return carry

        lax.fori_loop(0, rows // QB, block, 0)
        out_ref[1, :, part] = dk_ref[...].astype(BF)
        out_ref[2, :, part] = dv_ref[...].astype(BF)


def attend(project, mask):
    rows, columns = project.shape
    width = columns // 3
    pair = 2 * 64
    pairs = width // pair
    cost = pl.CostEstimate(
        flops=4 * rows * rows * width, bytes_accessed=8 * rows * width, transcendentals=0
    )
    return pl.pallas_call(
        forward_kernel,
        grid=(pairs,),
        in_specs=[
            pl.BlockSpec((rows, pair), lambda j: (0, j)),
            pl.BlockSpec((rows, pair), lambda j: (0, pairs + j)),
            pl.BlockSpec((rows, pair), lambda j: (0, 2 * pairs + j)),
            pl.BlockSpec((rows, QB), lambda j: (0, 0)),
        ],
        out_specs=[
            pl.BlockSpec((rows, pair), lambda j: (0, j)),
            pl.BlockSpec((1, 2, rows), lambda j: (j, 0, 0)),
        ],
        out_shape=[
            jax.ShapeDtypeStruct((rows, width), BF),
            jax.ShapeDtypeStruct((pairs, 2, rows), F32),
        ],
        cost_estimate=cost,
        name="attend",
    )(project, project, project, mask)


def attend_back(project, incoming, lse, mask):
    rows, columns = project.shape
    width = columns // 3
    pair = 2 * 64
    pairs = width // pair
    cost = pl.CostEstimate(
        flops=10 * rows * rows * width, bytes_accessed=14 * rows * width, transcendentals=0
    )
    return pl.pallas_call(
        backward_kernel,
        grid=(pairs,),
        in_specs=[
            pl.BlockSpec((rows, pair), lambda j: (0, j)),
            pl.BlockSpec((rows, pair), lambda j: (0, pairs + j)),
            pl.BlockSpec((rows, pair), lambda j: (0, 2 * pairs + j)),
            pl.BlockSpec((rows, pair), lambda j: (0, j)),
            pl.BlockSpec((1, 2, rows), lambda j: (j, 0, 0)),
            pl.BlockSpec((rows, QB), lambda j: (0, 0)),
        ],
        out_specs=pl.BlockSpec((3, rows, pair), lambda j: (0, 0, j)),
        out_shape=jax.ShapeDtypeStruct((3, rows, width), BF),
        scratch_shapes=[pltpu.VMEM((rows, pair // 2), F32), pltpu.VMEM((rows, pair // 2), F32)],
        cost_estimate=cost,
        name="attend_back",
    )(project, project, project, incoming, lse, mask)


def body(tokens, lengths, cotangent, w_qkv, w_out, w_up, w_down, *small):
    cells, rows_local, width = tokens.shape
    ya, xb, chips = size("ya"), size("xb"), size("seq")
    core, place = lax.axis_index("core"), lax.axis_index("seq")
    chip_pairs = ya * xb
    half = width // 2
    own_rows = chips * rows_local // 2
    sizes = [member.shape[0] for member in small]

    packed = lax.all_gather(jnp.concatenate(small)[None], ALL, axis=0, tiled=True)
    vectors, at = [], 0
    for count in sizes:
        vectors.append(packed[:, at : at + count].reshape(-1).astype(F32))
        at += count
    (
        gain_one, shift_one, bias_query, bias_value, bias_out,
        gain_two, shift_two, bias_up, bias_down,
    ) = vectors
    full_qkv = lax.all_gather(w_qkv, ALL, axis=0, tiled=True)
    qkv = pick(full_qkv.reshape(width, 3, 2, half), 2, core).reshape(width, 3 * half)
    out_full = lax.all_gather(w_out, ALL, axis=0, tiled=True)
    full_up = lax.all_gather(w_up, ALL, axis=0, tiled=True)
    hidden_all = full_up.shape[1]
    up = pick(full_up.reshape(width, chip_pairs, 2, -1), 2, core).reshape(width, hidden_all // 2)
    down = lax.all_gather(w_down, ("ya", "xb", "seq"), axis=0, tiled=True)
    up_bias = pick(bias_up.reshape(chip_pairs, 2, -1), 1, core).reshape(-1)
    project_bias = jnp.concatenate(
        [
            pick(bias_query.reshape(2, half), 0, core),
            jnp.zeros((half,), F32),
            pick(bias_value.reshape(2, half), 0, core),
        ]
    )

    inputs = to_cells(tokens)
    incoming = to_cells(cotangent)
    other_counts = swap(lengths)
    counts = jnp.where(core == 0, jnp.concatenate([lengths, other_counts]), jnp.concatenate([other_counts, lengths]))
    count = lax.dynamic_index_in_dim(counts, place, 0, keepdims=False)
    row = jnp.arange(2 * own_rows)
    holder = jnp.where(row < own_rows, core, 1 - core)
    row = row % own_rows
    position = (row // (rows_local // 2)) * rows_local + holder * (rows_local // 2) + row % (rows_local // 2)
    mask = jnp.broadcast_to((position < count).astype(F32)[:, None], (2 * own_rows, QB))

    inputs = inputs.astype(F32)
    normal_one, inverse_one = normalise(inputs)
    normed_low = (normal_one * gain_one + shift_one).astype(BF)
    normed_all = jnp.concatenate([normed_low, swap(normed_low)], axis=0)
    project = (dot(normed_all, qkv, NN) + project_bias).astype(BF)
    mixed_heads, lse = attend(project, mask)
    mixed_own = by_core(mixed_heads[:own_rows], swap(mixed_heads[own_rows:]), 1)
    middle = inputs + (dot(mixed_own, out_full, NN) + bias_out)
    normal_two, inverse_two = normalise(middle)
    second_low = (normal_two * gain_two + shift_two).astype(BF)
    second_all = jnp.concatenate([second_low, swap(second_low)], axis=0)
    hidden = dot(second_all, up, NN) + up_bias
    half_erf = 0.5 * (1.0 + lax.erf(hidden * (0.5**0.5)))
    active = (hidden * half_erf).astype(BF)
    slope = (half_erf + hidden * jnp.exp(-0.5 * hidden * hidden) * 0.3989422804014327).astype(BF)
    branch_own = dot(active[:own_rows], down, NN)
    branch_other = swap(dot(active[own_rows:], down, NN).astype(BF))
    output = (middle + (branch_own + branch_other.astype(F32) + bias_down)).astype(BF)
    output = from_cells(output, cells)

    incoming_all = jnp.concatenate([incoming, swap(incoming)], axis=0)
    grad_bias_down = jnp.sum(incoming.astype(F32), axis=0)
    d_hidden = (dot(incoming_all, down, NT) * slope.astype(F32)).astype(BF)
    grad_down = dot(active, incoming_all, TN, BF)
    grad_down = reduce_chips(grad_down.reshape(ya, xb, chips, -1, width), 0).astype(F32)
    grad_up = reduce_columns(dot(second_all, d_hidden, TN, BF), chip_pairs)
    grad_bias_up = jnp.sum(d_hidden.astype(F32), axis=0)
    d_second = dot(d_hidden[:own_rows], up, NT) + swap(
        dot(d_hidden[own_rows:], up, NT).astype(BF)
    ).astype(F32)
    d_middle = incoming.astype(F32) + norm_back(normal_two, inverse_two, d_second, gain_two)
    grad_gain_two = jnp.sum(d_second * normal_two, axis=0)
    grad_shift_two = jnp.sum(d_second, axis=0)
    d_attend = d_middle.astype(BF)
    grad_bias_out = jnp.sum(d_attend.astype(F32), axis=0)
    d_mixed = dot(d_attend, out_full, NT).astype(BF)
    low, high = d_mixed[:, :half], d_mixed[:, half:]
    d_mixed_heads = jnp.concatenate(
        [jnp.where(core == 0, low, high), swap(jnp.where(core == 0, high, low))], axis=0
    )
    d_project = attend_back(project, d_mixed_heads, lse, mask)

    low, high = d_attend[:, :half], d_attend[:, half:]
    d_attend_columns = jnp.concatenate(
        [jnp.where(core == 0, low, high), swap(jnp.where(core == 0, high, low))], axis=0
    )
    mixed_other = by_core(mixed_heads[own_rows:], swap(mixed_heads[:own_rows]), 1)
    mixed_all = jnp.concatenate([mixed_own, mixed_other], axis=0)
    grad_out = reduce_columns(dot(mixed_all, d_attend_columns, TN, BF), 1)

    sides = jnp.sum(d_project.astype(F32), axis=1)
    flat = jnp.concatenate([d_project[0], d_project[1], d_project[2]], axis=1)
    d_normed = dot(flat[:own_rows], qkv, NT) + swap(dot(flat[own_rows:], qkv, NT).astype(BF)).astype(F32)
    grad_qkv = reduce_columns(dot(normed_all, flat, TN, BF), 3)
    input_grad = d_middle + norm_back(normal_one, inverse_one, d_normed, gain_one)
    input_grad = from_cells(input_grad.astype(BF), cells).astype(F32)
    grad_gain_one = jnp.sum(d_normed * normal_one, axis=0)
    grad_shift_one = jnp.sum(d_normed, axis=0)

    own_half = (jnp.arange(2) == core).astype(F32)
    totals = (
        grad_gain_one,
        grad_shift_one,
        own_half[:, None] * sides[0],
        own_half[:, None] * sides[2],
        grad_bias_out,
        grad_gain_two,
        grad_shift_two,
        own_half[:, None] * grad_bias_up.reshape(chip_pairs, 1, -1),
        grad_bias_down,
    )
    packed = jnp.concatenate([total.reshape(ya, xb, 2, chips, -1) for total in totals], axis=-1)
    packed = reduce_axis(packed, 2, "core")
    packed = reduce_axis(packed, 0, "ya")
    packed = reduce_axis(packed, 0, "xb")
    packed = reduce_axis(packed, 0, "seq")
    smalls, at = [], 0
    for count in sizes:
        smalls.append(packed[at : at + count])
        at += count
    return (output, input_grad, grad_qkv, grad_out, grad_up, grad_down, *smalls)


def solution(mesh):
    pairs, chips = mesh.devices.shape[0] // 2, mesh.devices.shape[1]
    fine = Mesh(mesh.devices.reshape(pairs // 2, 2, 2, chips), ALL)
    rows = P(DP, "seq", None)
    matrix = P(ALL, None)
    vector = P(ALL)
    return jax.shard_map(
        body,
        mesh=fine,
        in_specs=(rows, P(DP), rows) + (matrix,) * 4 + (vector,) * 9,
        out_specs=(rows, rows) + (matrix,) * 4 + (vector,) * 9,
        check_vma=False,
    )
```

```python
import jax
import jax.numpy as jnp
from jax import lax
from jax.experimental import pallas as pl
from jax.experimental.pallas import tpu as pltpu
from jax.sharding import Mesh
from jax.sharding import PartitionSpec as P

HEADS = 20
EPSILON = 1e-05
NEG = -1000000000.0
QB = 256
BF = jnp.bfloat16
F32 = jnp.float32
ALL = ("ya", "xb", "core", "seq")
DP = ("ya", "xb", "core")


def dot(left, right, dims, out=F32):
    return lax.dot_general(left, right, (dims, ((), ())), preferred_element_type=out)


NN = ((1,), (0,))
NT = ((1,), (1,))
TN = ((0,), (0,))


def size(name):
    return lax.axis_size(name)


def swap(values):
    return lax.ppermute(values, "core", [(0, 1), (1, 0)])


def by_core(own, other, axis):
    low = jnp.concatenate([own, other], axis=axis)
    high = jnp.concatenate([other, own], axis=axis)
    return jnp.where(lax.axis_index("core") == 0, low, high)


def pick(values, axis, which):
    return lax.dynamic_index_in_dim(values, which, axis, keepdims=False)


def normalise(values):
    mean = jnp.mean(values, axis=-1, keepdims=True)
    centered = values - mean
    inverse = lax.rsqrt(jnp.mean(centered * centered, axis=-1, keepdims=True) + EPSILON)
    return centered * inverse, inverse


def norm_back(normal, inverse, incoming, gain):
    scaled = incoming * gain
    first = jnp.mean(scaled, axis=-1, keepdims=True)
    second = jnp.mean(scaled * normal, axis=-1, keepdims=True)
    return (scaled - first - normal * second) * inverse


def route(cells, chips, step):
    pairs = []
    for core in range(2):
        for place in range(chips):
            block = (place + step) % chips
            target = (block // cells) * chips + core * cells + block % cells
            pairs.append((core * chips + place, target))
    return pairs


def to_cells(values):
    cells, rows, width = values.shape
    chips = size("seq")
    core, place = lax.axis_index("core"), lax.axis_index("seq")
    blocks = values.reshape(cells, 2, rows // 2, width).transpose(1, 0, 2, 3)
    blocks = blocks.reshape(chips, rows // 2, width)
    mine = core * cells + place % cells
    parts = []
    for step in range(chips):
        piece = pick(blocks, 0, (place + step) % chips)
        parts.append(lax.ppermute(piece, ("core", "seq"), route(cells, chips, step)))
    result = jnp.zeros((chips, rows // 2, width), values.dtype)
    for step in range(chips):
        slot = (mine - step + chips) % chips
        result = lax.dynamic_update_slice_in_dim(result, parts[step][None], slot, 0)
    return result.reshape(chips * rows // 2, width)


def from_cells(values, cells):
    chips = size("seq")
    core, place = lax.axis_index("core"), lax.axis_index("seq")
    rows = 2 * values.shape[0] // chips
    width = values.shape[1]
    blocks = values.reshape(chips, rows // 2, width)
    mine = core * cells + place % cells
    result = jnp.zeros((chips, rows // 2, width), values.dtype)
    parts = []
    for step in range(chips):
        piece = pick(blocks, 0, (mine - step + chips) % chips)
        back = [(b, a) for a, b in route(cells, chips, step)]
        parts.append(lax.ppermute(piece, ("core", "seq"), back))
    for step in range(chips):
        slot = (place + step) % chips
        result = lax.dynamic_update_slice_in_dim(result, parts[step][None], slot, 0)
    result = result.reshape(2, cells, rows // 2, width).transpose(1, 0, 2, 3)
    return result.reshape(cells, rows, width)


def reduce_axis(values, axis, name):
    count = size(name)
    if count > 4:
        return lax.psum_scatter(values, name, scatter_dimension=axis, tiled=False)
    index = lax.axis_index(name)
    parts = []
    for step in range(1, count):
        piece = pick(values, axis, (index + step) % count)
        pairs = [(j, (j + step) % count) for j in range(count)]
        parts.append(lax.ppermute(piece, name, pairs))
    total = pick(values, axis, index).astype(F32)
    for part in parts:
        total = total + part.astype(F32)
    return total.astype(values.dtype)


def reduce_near(first, second):
    first = reduce_axis(reduce_axis(first, 0, "ya"), 0, "xb")
    second = reduce_axis(reduce_axis(second, 1, "xb"), 0, "ya")
    return [first, second]


def reduce_far(halves):
    return [reduce_axis(half, 0, "seq") for half in halves]


def columns_near(grad):
    ya, xb, chips = size("ya"), size("xb"), size("seq")
    rows = grad.shape[0] // (ya * xb * 2 * chips)
    grad = grad.reshape(ya, xb, 2, chips, rows, -1)
    return reduce_near(grad[:, :, 0], grad[:, :, 1])


def columns_own(halves, parts):
    rows = halves[0].shape[0]
    first = lax.axis_index("core") == 0
    own = jnp.where(first, halves[0], halves[1]).reshape(rows, parts, 1, -1)
    other = swap(jnp.where(first, halves[1], halves[0])).reshape(rows, parts, 1, -1)
    return by_core(own, other, 2).astype(F32)


def forward_kernel(q_ref, k_ref, v_ref, mask_ref, o_ref, lse_ref):
    rows, lanes = q_ref.shape
    dim = lanes // 2
    scale = dim ** (-0.5)
    parts = [slice(head * dim, (head + 1) * dim) for head in range(2)]
    turned = [v_ref[:, part].T for part in parts]

    def block(index, carry):
        start = pl.multiple_of(index * QB, QB)
        valid = mask_ref[...] > 0
        for head, part in enumerate(parts):
            queries = q_ref[pl.ds(start, QB), part] * BF(scale)
            scores = jnp.where(valid, dot(k_ref[:, part], queries, NT), NEG)
            top = jnp.max(scores, axis=0, keepdims=True)
            exponent = jnp.exp(scores - top)
            total = jnp.sum(exponent, axis=0, keepdims=True)
            mixed = dot(turned[head], exponent.astype(BF), NN) / total
            o_ref[pl.ds(start, QB), part] = mixed.T.astype(BF)
            lse_ref[0, head : head + 1, pl.ds(start, QB)] = top + jnp.log(total)
        return carry

    lax.fori_loop(0, rows // QB, block, 0)


def backward_kernel(q_ref, k_ref, v_ref, d_ref, lse_ref, mask_ref, out_ref, dk_ref, dv_ref):
    rows, lanes = q_ref.shape
    dim = lanes // 2
    scale = dim ** (-0.5)
    parts = [slice(head * dim, (head + 1) * dim) for head in range(2)]
    turned = [k_ref[:, part].T for part in parts]
    dk_ref[...] = jnp.zeros_like(dk_ref)
    dv_ref[...] = jnp.zeros_like(dv_ref)

    def block(index, carry):
        start = pl.multiple_of(index * QB, QB)
        valid = mask_ref[...] > 0
        for head, part in enumerate(parts):
            queries = q_ref[pl.ds(start, QB), part] * BF(scale)
            incoming = d_ref[pl.ds(start, QB), part]
            lse = lse_ref[0, head : head + 1, pl.ds(start, QB)]
            scores = jnp.where(valid, dot(k_ref[:, part], queries, NT), NEG)
            soft = jnp.exp(scores - lse)
            d_soft = dot(v_ref[:, part], incoming, NT)
            inner = jnp.sum(soft * d_soft, axis=0, keepdims=True)
            d_scores = (soft * (d_soft - inner)).astype(BF)
            dv_ref[head] += dot(soft.astype(BF), incoming, NN)
            dk_ref[head] += dot(d_scores, queries, NN)
            d_queries = dot(turned[head], d_scores, NN) * scale
            out_ref[0, pl.ds(start, QB), part] = d_queries.T.astype(BF)
        return carry

    lax.fori_loop(0, rows // QB, block, 0)
    for head, part in enumerate(parts):
        out_ref[1, :, part] = dk_ref[head].astype(BF)
        out_ref[2, :, part] = dv_ref[head].astype(BF)


def attend(project, mask):
    rows, columns = project.shape
    width = columns // 3
    pair = 2 * 64
    pairs = width // pair
    cost = pl.CostEstimate(
        flops=4 * rows * rows * width, bytes_accessed=8 * rows * width, transcendentals=0
    )
    return pl.pallas_call(
        forward_kernel,
        grid=(pairs,),
        in_specs=[
            pl.BlockSpec((rows, pair), lambda j: (0, j)),
            pl.BlockSpec((rows, pair), lambda j: (0, pairs + j)),
            pl.BlockSpec((rows, pair), lambda j: (0, 2 * pairs + j)),
            pl.BlockSpec((rows, QB), lambda j: (0, 0)),
        ],
        out_specs=[
            pl.BlockSpec((rows, pair), lambda j: (0, j)),
            pl.BlockSpec((1, 2, rows), lambda j: (j, 0, 0)),
        ],
        out_shape=[
            jax.ShapeDtypeStruct((rows, width), BF),
            jax.ShapeDtypeStruct((pairs, 2, rows), F32),
        ],
        cost_estimate=cost,
        name="attend",
    )(project, project, project, mask)


def attend_back(project, incoming, lse, mask, first, count):
    rows, columns = project.shape
    pair = 2 * 64
    pairs = columns // (3 * pair)
    width = count * pair
    cost = pl.CostEstimate(
        flops=10 * rows * rows * width, bytes_accessed=14 * rows * width, transcendentals=0
    )
    return pl.pallas_call(
        backward_kernel,
        grid=(count,),
        in_specs=[
            pl.BlockSpec((rows, pair), lambda j: (0, first + j)),
            pl.BlockSpec((rows, pair), lambda j: (0, pairs + first + j)),
            pl.BlockSpec((rows, pair), lambda j: (0, 2 * pairs + first + j)),
            pl.BlockSpec((rows, pair), lambda j: (0, first + j)),
            pl.BlockSpec((1, 2, rows), lambda j: (first + j, 0, 0)),
            pl.BlockSpec((rows, QB), lambda j: (0, 0)),
        ],
        out_specs=pl.BlockSpec((3, rows, pair), lambda j: (0, 0, j)),
        out_shape=jax.ShapeDtypeStruct((3, rows, width), BF),
        scratch_shapes=[pltpu.VMEM((2, rows, pair // 2), F32), pltpu.VMEM((2, rows, pair // 2), F32)],
        cost_estimate=cost,
        name="attend_back",
    )(project, project, project, incoming, lse, mask)


def gather_axis(values, name):
    count = size(name)
    index = lax.axis_index(name)
    if count > 4:
        return lax.all_gather(values, name, axis=0, tiled=False)
    result = jnp.zeros((count,) + values.shape, values.dtype)
    result = lax.dynamic_update_slice_in_dim(result, values[None], index, 0)
    for step in range(1, count):
        part = lax.ppermute(values, name, [(j, (j + step) % count) for j in range(count)])
        slot = (index - step + count) % count
        result = lax.dynamic_update_slice_in_dim(result, part[None], slot, 0)
    return result


def relative(values, name):
    count = size(name)
    parts = [values]
    for step in range(1, count):
        parts.append(lax.ppermute(values, name, [(j, (j + step) % count) for j in range(count)]))
    return parts


def lay_kernel(slots_ref, *refs):
    out_ref = refs[-1]
    side = len(out_ref.shape) == 3
    width = refs[0].shape[1]
    for index in range((len(refs) - 1) // 2):

        @pl.when(pl.program_id(0) == index)
        def _():
            if side:
                out_ref[0, :, :width] = refs[2 * index][...]
                out_ref[0, :, width:] = refs[2 * index + 1][...]
            else:
                out_ref[0, 0] = refs[2 * index][...]
                out_ref[0, 1] = refs[2 * index + 1][...]


def lay(first, second, slots, side):
    count = len(first)
    rows, width = first[0].shape
    block = (rows, 2 * width) if side else (2, rows, width)
    rest = (0,) * len(block)
    pieces = [piece for pair in zip(first, second) for piece in pair]
    whole = pl.BlockSpec((rows, width), lambda j, slots: (0, 0), pipeline_mode=pl.Buffered(1))
    return pl.pallas_call(
        lay_kernel,
        grid_spec=pltpu.PrefetchScalarGridSpec(
            num_scalar_prefetch=1,
            grid=(count,),
            in_specs=[whole] * (2 * count),
            out_specs=pl.BlockSpec((1,) + block, lambda j, slots: (slots[j],) + rest),
        ),
        out_shape=jax.ShapeDtypeStruct((count,) + block, first[0].dtype),
        cost_estimate=pl.CostEstimate(
            flops=0, bytes_accessed=8 * count * rows * width, transcendentals=0
        ),
        name="lay",
    )(slots, *pieces)


def gather_seq(values):
    done = gather_axis(values, "seq")
    chips, _, rows, width = done.shape
    return [done[:, half].reshape(chips * rows, width) for half in range(2)]


def gather_chips(halves, side=False):
    ya, xb = size("ya"), size("xb")
    ia, ib = lax.axis_index("ya"), lax.axis_index("xb")
    first = {}
    for b, part in enumerate(relative(halves[0], "xb")):
        for a, piece in enumerate(relative(part, "ya")):
            first[a, b] = piece
    second = {}
    for a, part in enumerate(relative(halves[1], "ya")):
        for b, piece in enumerate(relative(part, "xb")):
            second[a, b] = piece
    keys = sorted(first)
    slots = jnp.stack([((ia - a + ya) % ya) * xb + (ib - b + xb) % xb for a, b in keys])
    slots = slots.astype(jnp.int32)
    return lay([first[key] for key in keys], [second[key] for key in keys], slots, side)


def after(values, *others):
    return lax.optimization_barrier((values,) + others)[0]


def body(tokens, lengths, cotangent, w_qkv, w_out, w_up, w_down, *small):
    cells, rows_local, width = tokens.shape
    ya, xb, chips = size("ya"), size("xb"), size("seq")
    core, place = lax.axis_index("core"), lax.axis_index("seq")
    chip_pairs = ya * xb
    half = width // 2
    own_rows = chips * rows_local // 2
    sizes = [member.shape[0] for member in small]

    packed = gather_axis(gather_axis(gather_axis(gather_axis(jnp.concatenate(small), "seq"), "core"), "xb"), "ya")
    packed = packed.reshape(-1, sum(sizes))
    vectors, at = [], 0
    for count in sizes:
        vectors.append(packed[:, at : at + count].reshape(-1).astype(F32))
        at += count
    (
        gain_one, shift_one, bias_query, bias_value, bias_out,
        gain_two, shift_two, bias_up, bias_down,
    ) = vectors
    def columns(shard, parts):
        pieces = shard.reshape(shard.shape[0], parts, 2, -1)
        own = pick(pieces, 2, core).reshape(shard.shape[0], -1)
        other = swap(pick(pieces, 2, 1 - core).reshape(shard.shape[0], -1))
        return jnp.where(core == 0, jnp.stack([own, other]), jnp.stack([other, own]))

    hidden_half = w_up.shape[1] // 2
    inputs = to_cells(tokens)
    seq_qkv = gather_seq(columns(w_qkv, 3))
    seq_out = gather_seq(columns(w_out, 1))
    seq_up = gather_seq(after(columns(w_up, chip_pairs), seq_qkv[0]))
    shards = after(w_down, seq_up[0])
    seq_down = gather_seq(jnp.stack([shards[:, :half], shards[:, half:]]))
    incoming = to_cells(after(cotangent, seq_up[0]))
    qkv = gather_chips(seq_qkv).reshape(width, 3 * half)
    seq_out = after(seq_out, qkv)
    out_own = gather_chips(seq_out).reshape(width, half)
    out_other = swap(out_own)
    seq_up = after(seq_up, qkv)
    up = gather_chips(seq_up).reshape(width, hidden_half)
    seq_down = after(seq_down, up)
    down = gather_chips(seq_down, True).reshape(hidden_half, width)
    up_bias = pick(bias_up.reshape(chip_pairs, 2, -1), 1, core).reshape(-1)
    project_bias = jnp.concatenate(
        [
            pick(bias_query.reshape(2, half), 0, core),
            jnp.zeros((half,), F32),
            pick(bias_value.reshape(2, half), 0, core),
        ]
    )

    other_counts = swap(lengths)
    counts = jnp.where(core == 0, jnp.concatenate([lengths, other_counts]), jnp.concatenate([other_counts, lengths]))
    count = lax.dynamic_index_in_dim(counts, place, 0, keepdims=False)
    row = jnp.arange(2 * own_rows)
    holder = jnp.where(row < own_rows, core, 1 - core)
    row = row % own_rows
    position = (row // (rows_local // 2)) * rows_local + holder * (rows_local // 2) + row % (rows_local // 2)
    mask = jnp.broadcast_to((position < count).astype(F32)[:, None], (2 * own_rows, QB))

    inputs = inputs.astype(F32)
    normal_one, inverse_one = normalise(inputs)
    normed_low = (normal_one * gain_one + shift_one).astype(BF)
    normed_all = jnp.concatenate([normed_low, swap(normed_low)], axis=0)
    project = (dot(normed_all, qkv, NN) + project_bias).astype(BF)
    mixed_heads, lse = attend(project, mask)
    mixed_own = by_core(mixed_heads[:own_rows], swap(mixed_heads[own_rows:]), 1)
    attended = by_core(dot(mixed_own, out_own, NN), dot(mixed_own, out_other, NN), 1)
    middle = inputs + (attended + bias_out)
    normal_two, inverse_two = normalise(middle)
    second_low = (normal_two * gain_two + shift_two).astype(BF)
    second_all = jnp.concatenate([second_low, swap(second_low)], axis=0)
    hidden = dot(second_all, up, NN) + up_bias
    half_erf = 0.5 * (1.0 + lax.erf(hidden * (0.5**0.5)))
    active = (hidden * half_erf).astype(BF)
    slope = (half_erf + hidden * jnp.exp(-0.5 * hidden * hidden) * 0.3989422804014327).astype(BF)
    incoming_all = jnp.concatenate([incoming, swap(incoming)], axis=0)
    grad_down = dot(active, incoming_all, TN, BF)
    active = after(active, grad_down)
    grad_down = grad_down.reshape(ya, xb, chips, -1, width)
    near_down = reduce_near(grad_down[..., :half], grad_down[..., half:])
    far_down = reduce_far(near_down)
    branch_own = dot(active[:own_rows], down, NN)
    branch_other = swap(dot(active[own_rows:], down, NN).astype(BF))
    output = (middle + (branch_own + branch_other.astype(F32) + bias_down)).astype(BF)
    output = from_cells(output, cells)

    grad_bias_down = jnp.sum(incoming.astype(F32), axis=0)
    d_hidden = (dot(incoming_all, down, NT) * slope.astype(F32)).astype(BF)
    near_up = columns_near(dot(second_all, d_hidden, TN, BF))
    grad_bias_up = jnp.sum(d_hidden.astype(F32), axis=0)
    d_second = dot(d_hidden[:own_rows], up, NT) + swap(
        dot(d_hidden[own_rows:], up, NT).astype(BF)
    ).astype(F32)
    d_middle = incoming.astype(F32) + norm_back(normal_two, inverse_two, d_second, gain_two)
    grad_gain_two = jnp.sum(d_second * normal_two, axis=0)
    grad_shift_two = jnp.sum(d_second, axis=0)
    d_attend = d_middle.astype(BF)
    grad_bias_out = jnp.sum(d_attend.astype(F32), axis=0)
    low, high = d_attend[:, :half], d_attend[:, half:]
    d_attend_own = jnp.where(core == 0, low, high)
    d_attend_other = jnp.where(core == 0, high, low)
    d_mixed = (dot(d_attend_own, out_own, NT) + dot(d_attend_other, out_other, NT)).astype(BF)
    low, high = d_mixed[:, :half], d_mixed[:, half:]
    d_mixed_heads = jnp.concatenate(
        [jnp.where(core == 0, low, high), swap(jnp.where(core == 0, high, low))], axis=0
    )

    d_attend_columns = jnp.concatenate([d_attend_own, swap(d_attend_other)], axis=0)
    mixed_other = by_core(mixed_heads[own_rows:], swap(mixed_heads[:own_rows]), 1)
    mixed_all = jnp.concatenate([mixed_own, mixed_other], axis=0)
    near_out = columns_near(dot(mixed_all, d_attend_columns, TN, BF))

    pairs = half // 128
    front = (pairs + 1) // 2
    d_mixed_heads = after(d_mixed_heads, far_down)
    part = attend_back(project, d_mixed_heads, lse, mask, 0, front)
    flats = [jnp.concatenate([part[0], part[1], part[2]], axis=1)]
    far_up = reduce_far(near_up)
    near_qkv = [columns_near(dot(normed_all, flats[0], TN, BF))]
    d_mixed_heads = after(d_mixed_heads, near_up, near_out, flats[0])
    part_two = attend_back(project, d_mixed_heads, lse, mask, front, pairs - front)
    flats.append(jnp.concatenate([part_two[0], part_two[1], part_two[2]], axis=1))
    near_qkv.append(columns_near(dot(normed_all, flats[1], TN, BF)))
    far_out = reduce_far(near_out)

    d_project = jnp.concatenate([part, part_two], axis=2)
    sides = jnp.sum(d_project.astype(F32), axis=1)
    flat = jnp.concatenate([d_project[0], d_project[1], d_project[2]], axis=1)
    d_normed = dot(flat[:own_rows], qkv, NT) + swap(dot(flat[own_rows:], qkv, NT).astype(BF)).astype(F32)
    grad_down = jnp.concatenate(far_down, axis=-1).astype(F32)
    grad_up = columns_own(far_up, chip_pairs).reshape(w_up.shape)
    grad_out = columns_own(far_out, 1).reshape(w_out.shape)
    grad_qkv = [columns_own(reduce_far(near), 3) for near in near_qkv]
    grad_qkv = jnp.concatenate(grad_qkv, axis=-1).reshape(w_qkv.shape)
    input_grad = d_middle + norm_back(normal_one, inverse_one, d_normed, gain_one)
    input_grad = from_cells(input_grad.astype(BF), cells).astype(F32)
    grad_gain_one = jnp.sum(d_normed * normal_one, axis=0)
    grad_shift_one = jnp.sum(d_normed, axis=0)

    own_half = (jnp.arange(2) == core).astype(F32)
    totals = (
        grad_gain_one,
        grad_shift_one,
        own_half[:, None] * sides[0],
        own_half[:, None] * sides[2],
        grad_bias_out,
        grad_gain_two,
        grad_shift_two,
        own_half[:, None] * grad_bias_up.reshape(chip_pairs, 1, -1),
        grad_bias_down,
    )
    packed = jnp.concatenate([total.reshape(ya, xb, 2, chips, -1) for total in totals], axis=-1)
    packed = reduce_axis(packed, 2, "core")
    packed = reduce_axis(packed, 0, "ya")
    packed = reduce_axis(packed, 0, "xb")
    packed = reduce_axis(packed, 0, "seq")
    smalls, at = [], 0
    for count in sizes:
        smalls.append(packed[at : at + count])
        at += count
    return (output, input_grad, grad_qkv, grad_out, grad_up, grad_down, *smalls)


def solution(mesh):
    pairs, chips = mesh.devices.shape[0] // 2, mesh.devices.shape[1]
    fine = Mesh(mesh.devices.reshape(pairs // 2, 2, 2, chips), ALL)
    rows = P(DP, "seq", None)
    matrix = P(ALL, None)
    vector = P(ALL)
    return jax.shard_map(
        body,
        mesh=fine,
        in_specs=(rows, P(DP), rows) + (matrix,) * 4 + (vector,) * 9,
        out_specs=(rows, rows) + (matrix,) * 4 + (vector,) * 9,
        check_vma=False,
    )
```
